1024 devices in a mesh: seq: 128 (over y, z), head: 8 (over x, core).
Axes of the slice: x: 4, y: 4, z: 32, core: 2. Of those that a mesh axis runs over, the one named last changes fastest.
Arguments:
- queries: bfloat16 [16384, 2048], P('seq', 'head'), may hold values from -6 to 6
- keys: bfloat16 [16384, 2048], P('seq', 'head'), may hold values from -6 to 6
- values: bfloat16 [16384, 2048], P('seq', 'head'), may hold values from -6 to 6
- grad_out: bfloat16 [16384, 2048], P('seq', 'head'), may hold values from -6 to 6
Outputs:
- grad_queries: bfloat16 [16384, 2048], P(('seq', 'head'))
- grad_keys: bfloat16 [16384, 2048], P(('seq', 'head'))
- grad_values: bfloat16 [16384, 2048], P(('seq', 'head'))
The draws below stay inside these ranges and needn't reach their ends.
All inputs are finite; a program needn't handle non-finite values.
Results may differ from the reference program's by a relative error of at most 0.0049.
Values may be sent and summed in bfloat16 or wider, within the bound.
No kernel may reach another device: no remote copies, remote signals or barrier semaphores. Data moves between devices by JAX's collectives and lax.ppermute only.
A program may use at most 128 MiB of HBM per device.

```python
import math
import jax
import jax.numpy as jnp
from jax import lax

HEADS = 16
DH = 128
TOK_DEV = 128
LENGTH = 16384
N_SEQ = 128


def level_of(rng, extent, shards, low, high):
    gain = 1.0
    for dim, parts in shards:
        draws = jax.random.uniform(jax.random.fold_in(jax.random.fold_in(rng, 6), dim), (parts,), jnp.float32, low / len(shards), high / len(shards))
        gain = gain * jnp.repeat(jnp.exp(draws), extent[dim] // parts).reshape((-1,) + (1,) * (len(extent) - 1 - dim))
    return gain


def centred(stream_key, dims, deviation, reach, shards=(), kind=jnp.bfloat16):
    drawn = jax.random.normal(stream_key, dims, jnp.float32) * deviation
    if len(shards) > 0:
        drawn = level_of(stream_key, dims, shards, -0.22, 0.18) * drawn
    return jnp.clip(drawn, min=-reach, max=reach).astype(kind)


def setup_inputs(seed: int = 0) -> dict:
    key_of = jax.random.split(jax.random.key(seed), 5)
    return {
        "queries": centred(key_of[0], (LENGTH, HEADS * DH), 1.0, 6.0, ((0, 128), (1, 8))),
        "keys": centred(key_of[1], (LENGTH, HEADS * DH), 1.0, 6.0, ((0, 128), (1, 8))),
        "values": centred(key_of[2], (LENGTH, HEADS * DH), 1.0, 6.0, ((0, 128), (1, 8))),
        "grad_out": centred(key_of[3], (LENGTH, HEADS * DH), 1.0, 6.0, ((0, 128), (1, 8))),
    }


def reference(queries, keys, values, grad_out):
    scale = 1.0 / math.sqrt(DH * LENGTH)
    shape4 = (N_SEQ, TOK_DEV, HEADS, DH)
    q_all = queries.reshape(shape4).astype(jnp.float32)
    k_all = keys.reshape(shape4).astype(jnp.float32)
    v_all = values.reshape(shape4).astype(jnp.float32)
    g_all = grad_out.reshape(shape4).astype(jnp.float32)
    kv_all = scale * jnp.einsum('cthd,cthe->chde', k_all, v_all)
    qg_all = scale * jnp.einsum('cthd,cthe->chde', q_all, g_all)
    kv_incl = jnp.cumsum(kv_all, axis=0)
    qg_incl = jnp.cumsum(qg_all, axis=0)
    state_all = (kv_incl - kv_all).astype(jnp.bfloat16)
    later_all = (qg_incl[-1][None] - qg_incl).astype(jnp.bfloat16)
    rows = jnp.arange(TOK_DEV, dtype=jnp.int32)
    causal = rows[:, None] >= rows[None, :]

    def one_block(items):
        q_blk, k_blk, v_blk, g_blk, state, later = items
        state = state.astype(jnp.float32)
        later = later.astype(jnp.float32)
        scores = jnp.einsum('thd,shd->hts', q_blk, k_blk)
        grads = jnp.einsum('thd,shd->hts', g_blk, v_blk)
        probs = (scale * jnp.where(causal[None], scores, 0.0)).astype(jnp.bfloat16).astype(jnp.float32)
        dprobs = (scale * jnp.where(causal[None], grads, 0.0)).astype(jnp.bfloat16).astype(jnp.float32)
        d_query = jnp.einsum('hts,shd->thd', dprobs, k_blk) + jnp.einsum('the,hde->thd', g_blk, state)
        d_key = jnp.einsum('hts,thd->shd', dprobs, q_blk) + jnp.einsum('the,hde->thd', v_blk, later)
        d_value = jnp.einsum('hts,the->she', probs, g_blk) + jnp.einsum('thd,hde->the', k_blk, later)
        return (d_query.astype(jnp.bfloat16), d_key.astype(jnp.bfloat16), d_value.astype(jnp.bfloat16))
    d_query, d_key, d_value = lax.map(one_block, (q_all, k_all, v_all, g_all, state_all, later_all))
    flat = (LENGTH, HEADS * DH)
    return (d_query.reshape(flat), d_key.reshape(flat), d_value.reshape(flat))
```

```python
import math

import jax
import jax.numpy as jnp
import numpy as np
from jax import lax
from jax.sharding import Mesh, PartitionSpec as P

DH = 128
ROWS, QUADS, QUAD = 4, 8, 4
NEAR = ("row", "place")
BF16, F32 = jnp.bfloat16, jnp.float32


def dot(a, b, dims):
    return lax.dot_general(a, b, dims, preferred_element_type=F32)


def on_device(queries, keys, values, grad_out):
    tokens, width = queries.shape
    heads = width // DH
    shape3 = (tokens, heads, DH)
    q, k, v, g = (a.reshape(shape3) for a in (queries, keys, values, grad_out))
    length = tokens * ROWS * QUADS * QUAD
    scale = 1.0 / math.sqrt(DH * length)
    near = ROWS * QUAD
    part = DH // near

    kv = jnp.einsum("thd,the->hde", k, v, preferred_element_type=F32).astype(BF16)
    qg = jnp.einsum("thd,the->hde", q, g, preferred_element_type=F32).astype(BF16)

    pieces = jnp.stack([kv, qg]).reshape(2, heads, near, part, DH).transpose(2, 0, 1, 3, 4)
    with jax.named_scope("near_exchange"):
        pieces = lax.all_to_all(pieces, NEAR, 0, 0, tiled=True)
    pieces = pieces.reshape(ROWS, QUAD, 2, heads, part, DH).astype(F32)
    totals = pieces.sum(1).astype(BF16)
    sends = jnp.broadcast_to(totals[None], (QUADS,) + totals.shape)
    with jax.named_scope("far_exchange"):
        far = lax.all_to_all(sends, "quad", 0, 0, tiled=True)

    rows = jnp.arange(tokens, dtype=jnp.int32)
    causal = (rows[:, None] >= rows[None, :]).astype(F32) * scale
    scores = jnp.einsum("thd,shd->hts", q, k, preferred_element_type=F32)
    probs = (scores * causal[None]).astype(BF16)
    grads = jnp.einsum("thd,shd->hts", g, v, preferred_element_type=F32)
    dprobs = (grads * causal[None]).astype(BF16)
    dq = jnp.einsum("hts,shd->thd", dprobs, k, preferred_element_type=F32)
    dk = jnp.einsum("hts,thd->shd", dprobs, q, preferred_element_type=F32)
    dv = jnp.einsum("hts,the->she", probs, g, preferred_element_type=F32)

    far = far.astype(F32)
    mine = lax.axis_index("quad")
    index = jnp.arange(QUADS)
    before = (index < mine).astype(F32).reshape(QUADS, 1, 1, 1, 1)
    after = (index > mine).astype(F32).reshape(QUADS, 1, 1, 1, 1)
    kv_row = far[:, :, 0].sum(0)
    qg_row = far[:, :, 1].sum(0)
    kv_base = (far[:, :, 0] * before).sum(0)
    qg_base = (far[:, :, 1] * after).sum(0)
    outs = []
    for row in range(ROWS):
        kv_run = kv_base[row] + sum((kv_row[r] for r in range(row)), jnp.zeros_like(kv_row[0]))
        qg_run = qg_base[row] + sum((qg_row[r] for r in range(row + 1, ROWS)), jnp.zeros_like(qg_row[0]))
        kvs, qgs = [], []
        for place in range(QUAD):
            kvs.append(kv_run)
            kv_run = kv_run + pieces[row, place, 0]
        for place in reversed(range(QUAD)):
            qgs.append(qg_run)
            qg_run = qg_run + pieces[row, place, 1]
        outs += [jnp.stack([a, b]) for a, b in zip(kvs, qgs[::-1])]
    back = (jnp.stack(outs) * scale).astype(BF16)
    with jax.named_scope("near_return"):
        back = lax.all_to_all(back, NEAR, 0, 0, tiled=True)
    states = back.transpose(1, 2, 0, 3, 4).reshape(2, heads, DH, DH)
    state, later = states[0], states[1]

    dq = dq + jnp.einsum("the,hde->thd", g, state, preferred_element_type=F32)
    dk = dk + jnp.einsum("the,hde->thd", v, later, preferred_element_type=F32)
    dv = dv + jnp.einsum("thd,hde->the", k, later, preferred_element_type=F32)
    n_head = lax.axis_size(("x", "core"))
    own = tokens // n_head
    packed = jnp.stack([a.astype(BF16).reshape(n_head, own, width) for a in (dq, dk, dv)], axis=1)
    with jax.named_scope("heads_to_tokens"):
        packed = lax.all_to_all(packed, ("x", "core"), 0, 0, tiled=True)
    out = packed.transpose(1, 2, 0, 3).reshape(3, own, n_head * width)
    return out[0], out[1], out[2]


def solution(mesh):
    split = Mesh(
        np.asarray(mesh.devices).reshape(ROWS, QUADS, QUAD, 4, 2),
        ("row", "quad", "place", "x", "core"),
    )
    seq, head = ("row", "quad", "place"), ("x", "core")
    return jax.shard_map(
        on_device,
        mesh=split,
        in_specs=(P(seq, head),) * 4,
        out_specs=(P(seq + head, None),) * 3,
        check_vma=False,
    )
```

```python
import math

import jax
import jax.numpy as jnp
import numpy as np
from jax import lax
from jax.sharding import Mesh, PartitionSpec as P

DH = 128
ROWS, QUADS, QUAD = 4, 4, 8
NEAR = ("row", "place")
ROW_ORDER = [2, 3, 0, 1]
PLACE_ORDER = [4, 5, 6, 7, 0, 1, 2, 3]
FAR_ORDER = [2, 3, 0, 1]
NEAR_ORDER = [r * QUAD + p for r in ROW_ORDER for p in PLACE_ORDER]
BF16, F32 = jnp.bfloat16, jnp.float32


def on_device(queries, keys, values, grad_out):
    tokens, width = queries.shape
    heads = width // DH
    shape3 = (tokens, heads, DH)
    q, k, v, g = (a.reshape(shape3) for a in (queries, keys, values, grad_out))
    length = tokens * ROWS * QUADS * QUAD
    scale = 1.0 / math.sqrt(DH * length)
    near = ROWS * QUAD
    part = 8
    n_part = DH // part
    hs = near // n_part
    hh = heads // hs

    kv = jnp.einsum("thd,the->hde", k, v, preferred_element_type=F32).astype(BF16)
    qg = jnp.einsum("thd,the->hde", q, g, preferred_element_type=F32).astype(BF16)
    pieces = jnp.stack([kv, qg]).reshape(2, hs, hh, n_part, part, DH)
    pieces = pieces.transpose(1, 3, 0, 2, 4, 5).reshape(near, 2, hh, part, DH)
    with jax.named_scope("near_exchange"):
        pieces = lax.all_to_all(pieces, NEAR, 0, 0, tiled=True, axis_index_groups=[NEAR_ORDER])
    pieces = pieces.reshape(ROWS, QUAD, 2, hh, part, DH)
    pieces = pieces.astype(F32)
    totals = pieces.sum(1).astype(BF16)
    with jax.named_scope("far_exchange"):
        far = lax.all_to_all(jnp.broadcast_to(totals[None], (QUADS,) + totals.shape), "quad", 0, 0, tiled=True, axis_index_groups=[FAR_ORDER])

    rows = jnp.arange(tokens, dtype=jnp.int32)
    causal = (rows[:, None] >= rows[None, :]).astype(F32) * scale
    scores = jnp.einsum("thd,shd->hts", q, k, preferred_element_type=F32)
    probs = (scores * causal[None]).astype(BF16)
    grads = jnp.einsum("thd,shd->hts", g, v, preferred_element_type=F32)
    dprobs = (grads * causal[None]).astype(BF16)
    dq = jnp.einsum("hts,shd->thd", dprobs, k, preferred_element_type=F32)
    dk = jnp.einsum("hts,thd->shd", dprobs, q, preferred_element_type=F32)
    dv = jnp.einsum("hts,the->she", probs, g, preferred_element_type=F32)
    far, dq, dk, dv = lax.optimization_barrier((far, dq, dk, dv))

    far = far.astype(F32)
    mine = lax.axis_index("quad")
    index = jnp.array(FAR_ORDER)
    before = (index < mine).astype(F32).reshape(QUADS, 1, 1, 1, 1)
    after = (index > mine).astype(F32).reshape(QUADS, 1, 1, 1, 1)
    kv_row = far[:, :, 0].sum(0)
    qg_row = far[:, :, 1].sum(0)
    kv_base = (far[:, :, 0] * before).sum(0)
    qg_base = (far[:, :, 1] * after).sum(0)
    zero = jnp.zeros_like(kv_row[0])
    outs = {}
    for i, row in enumerate(ROW_ORDER):
        kv_run = kv_base[i] + sum((kv_row[j] for j, r in enumerate(ROW_ORDER) if r < row), zero)
        qg_run = qg_base[i] + sum((qg_row[j] for j, r in enumerate(ROW_ORDER) if r > row), zero)
        kvs, qgs = {}, {}
        for place in range(QUAD):
            kvs[place] = kv_run
            kv_run = kv_run + pieces[i, PLACE_ORDER.index(place), 0]
        for place in reversed(range(QUAD)):
            qgs[place] = qg_run
            qg_run = qg_run + pieces[i, PLACE_ORDER.index(place), 1]
        for j, place in enumerate(PLACE_ORDER):
            outs[i * QUAD + j] = jnp.stack([kvs[place], qgs[place]])
    back = (jnp.stack([outs[i] for i in range(near)]) * scale).astype(BF16)
    with jax.named_scope("near_return"):
        back = lax.all_to_all(back, NEAR, 0, 0, tiled=True, axis_index_groups=[NEAR_ORDER])
    states = back.reshape(hs, n_part, 2, hh, part, DH).transpose(2, 0, 3, 1, 4, 5).reshape(2, heads, DH, DH)
    state, later = states[0], states[1]

    dq = dq + jnp.einsum("the,hde->thd", g, state, preferred_element_type=F32)
    dk = dk + jnp.einsum("the,hde->thd", v, later, preferred_element_type=F32)
    dv = dv + jnp.einsum("thd,hde->the", k, later, preferred_element_type=F32)
    n_head = lax.axis_size(("x", "core"))
    own = tokens // n_head
    packed = jnp.stack([a.astype(BF16).reshape(n_head, own, width) for a in (dq, dk, dv)], axis=1)
    with jax.named_scope("heads_to_tokens"):
        packed = lax.all_to_all(packed, ("x", "core"), 0, 0, tiled=True)
    out = packed.transpose(1, 2, 0, 3).reshape(3, own, n_head * width)
    return out[0], out[1], out[2]


def solution(mesh):
    split = Mesh(
        np.asarray(mesh.devices).reshape(ROWS, QUADS, QUAD, 4, 2),
        ("row", "quad", "place", "x", "core"),
    )
    seq, head = ("row", "quad", "place"), ("x", "core")
    return jax.shard_map(
        on_device,
        mesh=split,
        in_specs=(P(seq, head),) * 4,
        out_specs=(P(seq + head, None),) * 3,
        check_vma=False,
    )
```

```python
import functools
import math

import jax
import jax.numpy as jnp
import numpy as np
from jax import lax
from jax.experimental import pallas as pl
from jax.experimental.pallas import tpu as pltpu
from jax.sharding import Mesh, PartitionSpec as P

DH = 128
ROWS, OCTS, OCT = 4, 4, 8
NEAR = ("row", "place")
ROW_ORDER = (2, 3, 0, 1)
PLACE_ORDER = (4, 5, 6, 7, 0, 1, 2, 3)
FAR_ORDER = (2, 3, 0, 1)
NEAR_ORDER = [r * OCT + p for r in ROW_ORDER for p in PLACE_ORDER]
BF16, F32 = jnp.bfloat16, jnp.float32
VMEM = pl.BlockSpec(memory_space=pltpu.VMEM)
HBM = pl.BlockSpec(memory_space=pl.ANY)


def dot(a, b, left, right):
    return lax.dot_general(a, b, (((left,), (right,)), ((), ())), preferred_element_type=F32)


def block_kernel(scale, q_in, k_in, v_in, g_in, pieces_ref, dq_ref, dk_ref, dv_ref, k_ref, v_ref, g_ref, q_ref, sems):
    copies = [
        pltpu.make_async_copy(src, dst, sems.at[n])
        for n, (src, dst) in enumerate(((k_in, k_ref), (v_in, v_ref), (q_in, q_ref), (g_in, g_ref)))
    ]
    for copy in copies:
        copy.start()
    tokens, width = q_ref.shape
    heads, parts = width // DH, DH // 8
    seen = lax.broadcasted_iota(jnp.int32, (tokens, tokens), 0) >= lax.broadcasted_iota(
        jnp.int32, (tokens, tokens), 1
    )
    copies[0].wait()
    copies[1].wait()
    for h in range(heads):
        cols = pl.ds(h * DH, DH)
        kv = dot(k_ref[:, cols], v_ref[:, cols], 0, 0)
        pieces_ref[h * parts : (h + 1) * parts, 0] = kv.reshape(parts, 8, DH).astype(BF16)
    copies[2].wait()
    copies[3].wait()
    for h in range(heads):
        cols = pl.ds(h * DH, DH)
        q, k, v, g = q_ref[:, cols], k_ref[:, cols], v_ref[:, cols], g_ref[:, cols]
        qg = dot(q, g, 0, 0)
        pieces_ref[h * parts : (h + 1) * parts, 1] = qg.reshape(parts, 8, DH).astype(BF16)
        probs = jnp.where(seen, dot(q, k, 1, 1) * scale, 0.0).astype(BF16)
        dprobs = jnp.where(seen, dot(g, v, 1, 1) * scale, 0.0).astype(BF16)
        dq_ref[:, cols] = dot(dprobs, k, 1, 0)
        dk_ref[:, cols] = dot(dprobs, q, 0, 0)
        dv_ref[:, cols] = dot(probs, g, 0, 0)


def totals_kernel(pieces_ref, sends_ref):
    for i in range(ROWS):
        for half in range(2):
            total = jnp.sum(pieces_ref[i * OCT : (i + 1) * OCT, half].astype(F32), axis=0).astype(BF16)
            for z in range(OCTS):
                sends_ref[z, i, half] = total


def prefix_kernel(scale, far_ref, pieces_ref, back_ref):
    mine = lax.axis_index("oct")
    kv_row, qg_row, kv_base, qg_base = [], [], [], []
    for i in range(ROWS):
        kv_all, qg_all, kv_some, qg_some = 0.0, 0.0, 0.0, 0.0
        for s, z in enumerate(FAR_ORDER):
            kv = far_ref[s, i, 0].astype(F32)
            qg = far_ref[s, i, 1].astype(F32)
            kv_all, qg_all = kv_all + kv, qg_all + qg
            kv_some = kv_some + jnp.where(z < mine, kv, 0.0)
            qg_some = qg_some + jnp.where(z > mine, qg, 0.0)
        kv_row.append(kv_all)
        qg_row.append(qg_all)
        kv_base.append(kv_some)
        qg_base.append(qg_some)
    for i, row in enumerate(ROW_ORDER):
        kv_run, qg_run = kv_base[i], qg_base[i]
        for j, other in enumerate(ROW_ORDER):
            if other < row:
                kv_run = kv_run + kv_row[j]
            if other > row:
                qg_run = qg_run + qg_row[j]
        for place in range(OCT):
            at = i * OCT + PLACE_ORDER.index(place)
            back_ref[at, 0] = (kv_run * scale).astype(BF16)
            kv_run = kv_run + pieces_ref[at, 0].astype(F32)
        for place in reversed(range(OCT)):
            at = i * OCT + PLACE_ORDER.index(place)
            back_ref[at, 1] = (qg_run * scale).astype(BF16)
            qg_run = qg_run + pieces_ref[at, 1].astype(F32)


def combine_kernel(back_ref, k_ref, v_ref, g_ref, dq_ref, dk_ref, dv_ref, packed_ref):
    tokens, width = k_ref.shape
    parts = DH // 8
    groups, own = packed_ref.shape[0], packed_ref.shape[1] // 3
    for h in range(width // DH):
        cols = pl.ds(h * DH, DH)
        state = back_ref[h * parts : (h + 1) * parts, 0].astype(F32).reshape(DH, DH).astype(BF16)
        later = back_ref[h * parts : (h + 1) * parts, 1].astype(F32).reshape(DH, DH).astype(BF16)
        dq = dq_ref[:, cols] + dot(g_ref[:, cols], state, 1, 1)
        dk = dk_ref[:, cols] + dot(v_ref[:, cols], later, 1, 1)
        dv = dv_ref[:, cols] + dot(k_ref[:, cols], later, 1, 0)
        for n, out in enumerate((dq, dk, dv)):
            packed_ref[:, n * own : (n + 1) * own, cols] = out.reshape(groups, own, DH).astype(BF16)


def spread_kernel(packed_ref, oq_ref, ok_ref, ov_ref, buf, sems):
    groups, rows, width = packed_ref.shape
    own = rows // 3
    copies = []
    for n, out in enumerate((oq_ref, ok_ref, ov_ref)):
        for j in range(groups):
            buf[n, :, j * width : (j + 1) * width] = packed_ref[j, n * own : (n + 1) * own, :]
        copy = pltpu.make_async_copy(buf.at[n], out, sems.at[n])
        copy.start()
        copies.append(copy)
    for copy in copies:
        copy.wait()


def inv(x):
    return pltpu.with_memory_space_constraint(x, pltpu.VMEM)


def call(kernel, ins, outs, in_specs=None, out_specs=None, **kw):
    return pl.pallas_call(
        kernel,
        out_shape=outs,
        in_specs=in_specs or [VMEM] * len(ins),
        out_specs=out_specs or jax.tree.map(lambda _: VMEM, outs),
        **kw,
    )(*ins)


def on_device(q, k, v, g):
    tokens, width = q.shape
    heads = width // DH
    length = tokens * ROWS * OCTS * OCT
    scale = 1.0 / math.sqrt(DH * length)
    near = ROWS * OCT
    shape = lambda s, t: jax.ShapeDtypeStruct(s, t)
    vshape = lambda s, t: pltpu.VMEM(s, t)

    local, bf = vshape((tokens, width), F32), vshape((tokens, width), BF16)
    pieces, dq, dk, dv, k, v, g = call(
        functools.partial(block_kernel, scale),
        (q, k, v, g),
        (vshape((near, 2, 8, DH), BF16),) + (local,) * 3 + (bf,) * 3,
        in_specs=[HBM] * 4,
        scratch_shapes=[pltpu.VMEM((tokens, width), BF16), pltpu.SemaphoreType.DMA((4,))],
    )
    with jax.named_scope("near_exchange"):
        pieces = lax.all_to_all(pieces, NEAR, 0, 0, tiled=True, axis_index_groups=[NEAR_ORDER])
    sends = call(totals_kernel, (inv(pieces),), vshape((OCTS, ROWS, 2, 8, DH), BF16))
    with jax.named_scope("far_exchange"):
        far = lax.all_to_all(sends, "oct", 0, 0, tiled=True, axis_index_groups=[FAR_ORDER])
    back = call(
        functools.partial(prefix_kernel, scale),
        (inv(far), inv(pieces)),
        vshape((near, 2, 8, DH), BF16),
    )
    with jax.named_scope("near_return"):
        back = lax.all_to_all(back, NEAR, 0, 0, tiled=True, axis_index_groups=[NEAR_ORDER])
    groups = lax.axis_size(("x", "core"))
    own = tokens // groups
    packed = call(combine_kernel, (inv(back), inv(k), inv(v), inv(g), inv(dq), inv(dk), inv(dv)), vshape((groups, 3 * own, width), BF16))
    with jax.named_scope("heads_to_tokens"):
        packed = lax.all_to_all(packed, ("x", "core"), 0, 0, tiled=True)
    out = shape((own, groups * width), BF16)
    return call(
        spread_kernel,
        (inv(packed),),
        (out,) * 3,
        out_specs=(HBM,) * 3,
        scratch_shapes=[pltpu.VMEM((3, own, groups * width), BF16), pltpu.SemaphoreType.DMA((3,))],
    )


def solution(mesh):
    split = Mesh(
        np.asarray(mesh.devices).reshape(ROWS, OCTS, OCT, 4, 2),
        ("row", "oct", "place", "x", "core"),
    )
    seq, head = ("row", "oct", "place"), ("x", "core")
    return jax.shard_map(
        on_device,
        mesh=split,
        in_specs=(P(seq, head),) * 4,
        out_specs=(P(seq + head, None),) * 3,
        check_vma=False,
    )
```

```python
import functools
import math

import jax
import jax.numpy as jnp
import numpy as np
from jax import lax
from jax.experimental import pallas as pl
from jax.experimental.pallas import tpu as pltpu
from jax.sharding import Mesh, PartitionSpec as P

DH = 128
ROWS, OCTS, OCT = 4, 4, 8
NEAR = ("row", "place")
ROW_ORDER = (2, 3, 0, 1)
PLACE_ORDER = (4, 5, 6, 7, 0, 1, 2, 3)
FAR_ORDER = (2, 3, 0, 1)
LATE = 2
HEAD_ORDER = (4, 5, 6, 7, 0, 1, 2, 3)
NEAR_ORDER = [r * OCT + p for r in ROW_ORDER for p in PLACE_ORDER]
BF16, F32 = jnp.bfloat16, jnp.float32
VMEM = pl.BlockSpec(memory_space=pltpu.VMEM)
HBM = pl.BlockSpec(memory_space=pl.ANY)


def dot(a, b, left, right):
    return lax.dot_general(a, b, (((left,), (right,)), ((), ())), preferred_element_type=F32)


def local_terms(scale, q, k, v, g):
    shape = (q.shape[0], q.shape[0])
    seen = lax.broadcasted_iota(jnp.int32, shape, 0) >= lax.broadcasted_iota(jnp.int32, shape, 1)
    probs = jnp.where(seen, dot(q, k, 1, 1) * scale, 0.0).astype(BF16)
    dprobs = jnp.where(seen, dot(g, v, 1, 1) * scale, 0.0).astype(BF16)
    return dot(dprobs, k, 1, 0), dot(dprobs, q, 0, 0), dot(probs, g, 0, 0)


def block_kernel(scale, q_in, k_in, v_in, g_in, pieces_ref, *rest):
    grads, (q_ref, k_ref, v_ref, g_ref), sems = rest[:3], rest[3:7], rest[7]
    copies = [
        pltpu.make_async_copy(src, dst, sems.at[n])
        for n, (src, dst) in enumerate(((k_in, k_ref), (v_in, v_ref), (q_in, q_ref), (g_in, g_ref)))
    ]
    for copy in copies:
        copy.start()
    heads, parts = q_ref.shape[1] // DH, DH // 8
    for half, (a_ref, b_ref) in enumerate(((k_ref, v_ref), (q_ref, g_ref))):
        copies[2 * half].wait()
        copies[2 * half + 1].wait()
        for h in range(heads):
            cols = pl.ds(h * DH, DH)
            out = dot(a_ref[:, cols], b_ref[:, cols], 0, 0)
            pieces_ref[h * parts : (h + 1) * parts, half] = out.reshape(parts, 8, DH).astype(BF16)

    @pl.when(lax.axis_index("oct") < LATE)
    def _():
        for h in range(heads):
            cols = pl.ds(h * DH, DH)
            terms = local_terms(scale, q_ref[:, cols], k_ref[:, cols], v_ref[:, cols], g_ref[:, cols])
            for ref, term in zip(grads, terms):
                ref[:, cols] = term


def totals_kernel(pieces_ref, sends_ref):
    mine = lax.axis_index("oct")
    kv, qg = [None] * ROWS, [None] * ROWS
    for i, row in enumerate(ROW_ORDER):
        kv[row] = jnp.sum(pieces_ref[i * OCT : (i + 1) * OCT, 0].astype(F32), axis=0)
        qg[row] = jnp.sum(pieces_ref[i * OCT : (i + 1) * OCT, 1].astype(F32), axis=0)
    kv_up, qg_down = kv[:1], qg[-1:]
    for row in range(1, ROWS):
        kv_up.append(kv_up[-1] + kv[row])
        qg_down.insert(0, qg[ROWS - 1 - row] + qg_down[0])
    to_later = [a.astype(BF16) for a in kv_up + qg_down[1:]]
    to_earlier = [a.astype(BF16) for a in kv_up[:-1] + qg_down]
    for s, z in enumerate(FAR_ORDER):
        @pl.when(mine < z)
        def _():
            for n, a in enumerate(to_later):
                sends_ref[s, n] = a

        @pl.when(mine >= z)
        def _():
            for n, a in enumerate(to_earlier):
                sends_ref[s, n] = a


def prefix_kernel(scale, far_ref, pieces_ref, back_ref):
    mine = lax.axis_index("oct")
    kv_far, qg_far = [0.0] * ROWS, [0.0] * ROWS
    for s, z in enumerate(FAR_ORDER):
        slots = [far_ref[s, n].astype(F32) for n in range(2 * ROWS - 1)]
        earlier, later = z < mine, z > mine
        for row in range(ROWS):
            kv = jnp.where(earlier, slots[row], 0.0)
            qg = jnp.where(later, slots[ROWS - 1 + row], 0.0)
            if row > 0:
                kv = jnp.where(later, slots[row - 1], kv)
            if row < ROWS - 1:
                qg = jnp.where(earlier, slots[ROWS + row], qg)
            kv_far[row], qg_far[row] = kv_far[row] + kv, qg_far[row] + qg
    order = [ROW_ORDER.index(row) * OCT for row in range(ROWS)]
    own = 0.0
    for row in range(ROWS):
        for place in range(OCT):
            at = order[row] + PLACE_ORDER.index(place)
            back_ref[at, 0] = ((kv_far[row] + own) * scale).astype(BF16)
            own = own + pieces_ref[at, 0].astype(F32)
    own = 0.0
    for row in reversed(range(ROWS)):
        for place in reversed(range(OCT)):
            at = order[row] + PLACE_ORDER.index(place)
            back_ref[at, 1] = ((qg_far[row] + own) * scale).astype(BF16)
            own = own + pieces_ref[at, 1].astype(F32)


def combine_kernel(scale, back_ref, q_ref, k_ref, v_ref, g_ref, dq_ref, dk_ref, dv_ref, packed_ref):
    tokens, width = k_ref.shape
    parts = DH // 8
    groups, own = packed_ref.shape[0], packed_ref.shape[1] // 3

    def head(h, local):
        cols = pl.ds(h * DH, DH)
        k, v, g = k_ref[:, cols], v_ref[:, cols], g_ref[:, cols]
        state = back_ref[h * parts : (h + 1) * parts, 0].astype(F32).reshape(DH, DH).astype(BF16)
        later = back_ref[h * parts : (h + 1) * parts, 1].astype(F32).reshape(DH, DH).astype(BF16)
        far = dot(g, state, 1, 1), dot(v, later, 1, 1), dot(k, later, 1, 0)
        for n, (a, b) in enumerate(zip(local, far)):
            out = (a + b).reshape(groups, own, DH).astype(BF16)
            for i, j in enumerate(HEAD_ORDER):
                packed_ref[i, n * own : (n + 1) * own, cols] = out[j]

    late = lax.axis_index("oct") >= LATE

    @pl.when(late)
    def _():
        for h in range(width // DH):
            cols = pl.ds(h * DH, DH)
            head(h, local_terms(scale, q_ref[:, cols], k_ref[:, cols], v_ref[:, cols], g_ref[:, cols]))

    @pl.when(jnp.logical_not(late))
    def _():
        for h in range(width // DH):
            cols = pl.ds(h * DH, DH)
            head(h, (dq_ref[:, cols], dk_ref[:, cols], dv_ref[:, cols]))


def spread_kernel(packed_ref, oq_ref, ok_ref, ov_ref, buf, sems):
    groups, rows, width = packed_ref.shape
    own = rows // 3
    copies = []
    for n, out in enumerate((oq_ref, ok_ref, ov_ref)):
        for i, j in enumerate(HEAD_ORDER):
            buf[n, :, j * width : (j + 1) * width] = packed_ref[i, n * own : (n + 1) * own, :]
        copy = pltpu.make_async_copy(buf.at[n], out, sems.at[n])
        copy.start()
        copies.append(copy)
    for copy in copies:
        copy.wait()


def inv(x):
    return pltpu.with_memory_space_constraint(x, pltpu.VMEM)


def call(kernel, ins, outs, in_specs=None, out_specs=None, **kw):
    return pl.pallas_call(
        kernel,
        out_shape=outs,
        in_specs=in_specs or [VMEM] * len(ins),
        out_specs=out_specs or jax.tree.map(lambda _: VMEM, outs),
        **kw,
    )(*ins)


def on_device(q, k, v, g):
    tokens, width = q.shape
    heads = width // DH
    length = tokens * ROWS * OCTS * OCT
    scale = 1.0 / math.sqrt(DH * length)
    near = ROWS * OCT
    shape = lambda s, t: jax.ShapeDtypeStruct(s, t)
    vshape = lambda s, t: pltpu.VMEM(s, t)

    local, bf = vshape((tokens, width), F32), vshape((tokens, width), BF16)
    pieces, dq, dk, dv, q, k, v, g = call(
        functools.partial(block_kernel, scale),
        (q, k, v, g),
        (vshape((near, 2, 8, DH), BF16),) + (local,) * 3 + (bf,) * 4,
        in_specs=[HBM] * 4,
        scratch_shapes=[pltpu.SemaphoreType.DMA((4,))],
    )
    with jax.named_scope("near_exchange"):
        pieces = lax.all_to_all(pieces, NEAR, 0, 0, tiled=True, axis_index_groups=[NEAR_ORDER])
    sends = call(totals_kernel, (inv(pieces),), vshape((OCTS, 2 * ROWS - 1, 8, DH), BF16))
    with jax.named_scope("far_exchange"):
        far = lax.all_to_all(sends, "oct", 0, 0, tiled=True, axis_index_groups=[FAR_ORDER])
    back = call(
        functools.partial(prefix_kernel, scale),
        (inv(far), inv(pieces)),
        vshape((near, 2, 8, DH), BF16),
    )
    with jax.named_scope("near_return"):
        back = lax.all_to_all(back, NEAR, 0, 0, tiled=True, axis_index_groups=[NEAR_ORDER])
    groups = lax.axis_size(("x", "core"))
    own = tokens // groups
    packed = call(functools.partial(combine_kernel, scale), tuple(map(inv, (back, q, k, v, g, dq, dk, dv))), vshape((groups, 3 * own, width), BF16))
    with jax.named_scope("heads_to_tokens"):
        packed = lax.all_to_all(packed, ("x", "core"), 0, 0, tiled=True, axis_index_groups=[HEAD_ORDER])
    out = shape((own, groups * width), BF16)
    return call(
        spread_kernel,
        (inv(packed),),
        (out,) * 3,
        out_specs=(HBM,) * 3,
        scratch_shapes=[pltpu.VMEM((3, own, groups * width), BF16), pltpu.SemaphoreType.DMA((3,))],
    )


def solution(mesh):
    split = Mesh(
        np.asarray(mesh.devices).reshape(ROWS, OCTS, OCT, 4, 2),
        ("row", "oct", "place", "x", "core"),
    )
    seq, head = ("row", "oct", "place"), ("x", "core")
    return jax.shard_map(
        on_device,
        mesh=split,
        in_specs=(P(seq, head),) * 4,
        out_specs=(P(seq + head, None),) * 3,
        check_vma=False,
    )
```

```python
import functools
import math

import jax
import jax.numpy as jnp
import numpy as np
from jax import lax
from jax.experimental import pallas as pl
from jax.experimental.pallas import tpu as pltpu
from jax.sharding import Mesh, PartitionSpec as P

DH = 128
ROWS, OCTS, OCT = 4, 4, 8
NEAR = ("row", "place")
ROW_ORDER = (2, 3, 0, 1)
PLACE_ORDER = (4, 3, 5, 2, 6, 1, 7, 0)
FAR_ORDER = (2, 0, 3, 1)
LATE = 2
HEAD_ORDER = (4, 5, 2, 3, 0, 1, 6, 7)
NEAR_ORDER = [r * OCT + p for r in ROW_ORDER for p in PLACE_ORDER]
BF16, F32 = jnp.bfloat16, jnp.float32
VMEM = pl.BlockSpec(memory_space=pltpu.VMEM)
HBM = pl.BlockSpec(memory_space=pl.ANY)


def dot(a, b, left, right):
    return lax.dot_general(a, b, (((left,), (right,)), ((), ())), preferred_element_type=F32)


def local_terms(scale, q, k, v, g):
    shape = (q.shape[0], q.shape[0])
    seen = lax.broadcasted_iota(jnp.int32, shape, 0) >= lax.broadcasted_iota(jnp.int32, shape, 1)
    probs = jnp.where(seen, dot(q, k, 1, 1) * scale, 0.0).astype(BF16)
    dprobs = jnp.where(seen, dot(g, v, 1, 1) * scale, 0.0).astype(BF16)
    return dot(dprobs, k, 1, 0), dot(dprobs, q, 0, 0), dot(probs, g, 0, 0)


def block_kernel(scale, q_in, k_in, v_in, g_in, pieces_ref, *rest):
    grads, (q_ref, k_ref, v_ref, g_ref), sems = rest[:3], rest[3:7], rest[7]
    copies = [
        pltpu.make_async_copy(src, dst, sems.at[n])
        for n, (src, dst) in enumerate(((k_in, k_ref), (v_in, v_ref), (q_in, q_ref), (g_in, g_ref)))
    ]
    for copy in copies:
        copy.start()
    heads, parts = q_ref.shape[1] // DH, DH // 8
    for half, (a_ref, b_ref) in enumerate(((k_ref, v_ref), (q_ref, g_ref))):
        copies[2 * half].wait()
        copies[2 * half + 1].wait()
        for h in range(heads):
            cols = pl.ds(h * DH, DH)
            out = dot(a_ref[:, cols], b_ref[:, cols], 0, 0)
            pieces_ref[h * parts : (h + 1) * parts, half] = out.reshape(parts, 8, DH).astype(BF16)

    @pl.when(lax.axis_index("oct") < LATE)
    def _():
        for h in range(heads):
            cols = pl.ds(h * DH, DH)
            terms = local_terms(scale, q_ref[:, cols], k_ref[:, cols], v_ref[:, cols], g_ref[:, cols])
            for ref, term in zip(grads, terms):
                ref[:, cols] = term


def totals_kernel(pieces_ref, sends_ref):
    mine = lax.axis_index("oct")
    kv, qg = [None] * ROWS, [None] * ROWS
    for i, row in enumerate(ROW_ORDER):
        kv[row] = jnp.sum(pieces_ref[i * OCT : (i + 1) * OCT, 0].astype(F32), axis=0)
        qg[row] = jnp.sum(pieces_ref[i * OCT : (i + 1) * OCT, 1].astype(F32), axis=0)
    kv_up, qg_down = kv[:1], qg[-1:]
    for row in range(1, ROWS):
        kv_up.append(kv_up[-1] + kv[row])
        qg_down.insert(0, qg[ROWS - 1 - row] + qg_down[0])
    to_later = [a.astype(BF16) for a in kv_up + qg_down[1:]]
    to_earlier = [a.astype(BF16) for a in kv_up[:-1] + qg_down]
    for s, z in enumerate(FAR_ORDER):
        @pl.when(mine < z)
        def _():
            for n, a in enumerate(to_later):
                sends_ref[s, n] = a

        @pl.when(mine >= z)
        def _():
            for n, a in enumerate(to_earlier):
                sends_ref[s, n] = a


def prefix_kernel(scale, far_ref, pieces_ref, back_ref):
    mine = lax.axis_index("oct")
    kv_far, qg_far = [0.0] * ROWS, [0.0] * ROWS
    for s, z in enumerate(FAR_ORDER):
        slots = [far_ref[s, n].astype(F32) for n in range(2 * ROWS - 1)]
        earlier, later = z < mine, z > mine
        for row in range(ROWS):
            kv = jnp.where(earlier, slots[row], 0.0)
            qg = jnp.where(later, slots[ROWS - 1 + row], 0.0)
            if row > 0:
                kv = jnp.where(later, slots[row - 1], kv)
            if row < ROWS - 1:
                qg = jnp.where(earlier, slots[ROWS + row], qg)
            kv_far[row], qg_far[row] = kv_far[row] + kv, qg_far[row] + qg
    order = [ROW_ORDER.index(row) * OCT for row in range(ROWS)]
    own = 0.0
    for row in range(ROWS):
        for place in range(OCT):
            at = order[row] + PLACE_ORDER.index(place)
            back_ref[at, 0] = ((kv_far[row] + own) * scale).astype(BF16)
            own = own + pieces_ref[at, 0].astype(F32)
    own = 0.0
    for row in reversed(range(ROWS)):
        for place in reversed(range(OCT)):
            at = order[row] + PLACE_ORDER.index(place)
            back_ref[at, 1] = ((qg_far[row] + own) * scale).astype(BF16)
            own = own + pieces_ref[at, 1].astype(F32)


def combine_kernel(scale, back_ref, q_ref, k_ref, v_ref, g_ref, dq_ref, dk_ref, dv_ref, packed_ref):
    tokens, width = k_ref.shape
    parts = DH // 8
    groups, own = packed_ref.shape[0], packed_ref.shape[1] // 3

    def head(h, local):
        cols = pl.ds(h * DH, DH)
        k, v, g = k_ref[:, cols], v_ref[:, cols], g_ref[:, cols]
        state = back_ref[h * parts : (h + 1) * parts, 0].astype(F32).reshape(DH, DH).astype(BF16)
        later = back_ref[h * parts : (h + 1) * parts, 1].astype(F32).reshape(DH, DH).astype(BF16)
        far = dot(g, state, 1, 1), dot(v, later, 1, 1), dot(k, later, 1, 0)
        for n, (a, b) in enumerate(zip(local, far)):
            out = (a + b).reshape(groups, own, DH).astype(BF16)
            for i, j in enumerate(HEAD_ORDER):
                packed_ref[i, n * own : (n + 1) * own, cols] = out[j]

    late = lax.axis_index("oct") >= LATE

    @pl.when(late)
    def _():
        for h in range(width // DH):
            cols = pl.ds(h * DH, DH)
            head(h, local_terms(scale, q_ref[:, cols], k_ref[:, cols], v_ref[:, cols], g_ref[:, cols]))

    @pl.when(jnp.logical_not(late))
    def _():
        for h in range(width // DH):
            cols = pl.ds(h * DH, DH)
            head(h, (dq_ref[:, cols], dk_ref[:, cols], dv_ref[:, cols]))


def spread_kernel(packed_ref, oq_ref, ok_ref, ov_ref, buf, sems):
    groups, rows, width = packed_ref.shape
    own = rows // 3
    copies = []
    for n, out in enumerate((oq_ref, ok_ref, ov_ref)):
        for i, j in enumerate(HEAD_ORDER):
            buf[n, :, j * width : (j + 1) * width] = packed_ref[i, n * own : (n + 1) * own, :]
        copy = pltpu.make_async_copy(buf.at[n], out, sems.at[n])
        copy.start()
        copies.append(copy)
    for copy in copies:
        copy.wait()


def inv(x):
    return pltpu.with_memory_space_constraint(x, pltpu.VMEM)


def call(kernel, ins, outs, in_specs=None, out_specs=None, **kw):
    return pl.pallas_call(
        kernel,
        out_shape=outs,
        in_specs=in_specs or [VMEM] * len(ins),
        out_specs=out_specs or jax.tree.map(lambda _: VMEM, outs),
        **kw,
    )(*ins)


def on_device(q, k, v, g):
    tokens, width = q.shape
    heads = width // DH
    length = tokens * ROWS * OCTS * OCT
    scale = 1.0 / math.sqrt(DH * length)
    near = ROWS * OCT
    shape = lambda s, t: jax.ShapeDtypeStruct(s, t)
    vshape = lambda s, t: pltpu.VMEM(s, t)

    local, bf = vshape((tokens, width), F32), vshape((tokens, width), BF16)
    pieces, dq, dk, dv, q, k, v, g = call(
        functools.partial(block_kernel, scale),
        (q, k, v, g),
        (vshape((near, 2, 8, DH), BF16),) + (local,) * 3 + (bf,) * 4,
        in_specs=[HBM] * 4,
        scratch_shapes=[pltpu.SemaphoreType.DMA((4,))],
    )
    with jax.named_scope("near_exchange"):
        pieces = lax.all_to_all(pieces, NEAR, 0, 0, tiled=True, axis_index_groups=[NEAR_ORDER])
    sends = call(totals_kernel, (inv(pieces),), vshape((OCTS, 2 * ROWS - 1, 8, DH), BF16))
    with jax.named_scope("far_exchange"):
        far = lax.all_to_all(sends, "oct", 0, 0, tiled=True, axis_index_groups=[FAR_ORDER])
    back = call(
        functools.partial(prefix_kernel, scale),
        (inv(far), inv(pieces)),
        vshape((near, 2, 8, DH), BF16),
    )
    with jax.named_scope("near_return"):
        back = lax.all_to_all(back, NEAR, 0, 0, tiled=True, axis_index_groups=[NEAR_ORDER])
    groups = lax.axis_size(("x", "core"))
    own = tokens // groups
    packed = call(functools.partial(combine_kernel, scale), tuple(map(inv, (back, q, k, v, g, dq, dk, dv))), vshape((groups, 3 * own, width), BF16))
    with jax.named_scope("heads_to_tokens"):
        packed = lax.all_to_all(packed, ("x", "core"), 0, 0, tiled=True, axis_index_groups=[HEAD_ORDER])
    out = shape((own, groups * width), BF16)
    return call(
        spread_kernel,
        (inv(packed),),
        (out,) * 3,
        out_specs=(HBM,) * 3,
        scratch_shapes=[pltpu.VMEM((3, own, groups * width), BF16), pltpu.SemaphoreType.DMA((3,))],
    )


def solution(mesh):
    split = Mesh(
        np.asarray(mesh.devices).reshape(ROWS, OCTS, OCT, 4, 2),
        ("row", "oct", "place", "x", "core"),
    )
    seq, head = ("row", "oct", "place"), ("x", "core")
    return jax.shard_map(
        on_device,
        mesh=split,
        in_specs=(P(seq, head),) * 4,
        out_specs=(P(seq + head, None),) * 3,
        check_vma=False,
    )
```

```python
import functools
import math

import jax
import jax.numpy as jnp
import numpy as np
from jax import lax
from jax.experimental import pallas as pl
from jax.experimental.pallas import tpu as pltpu
from jax.sharding import Mesh, PartitionSpec as P

DH = 128
ROWS, OCTS, OCT = 4, 4, 8
NEAR = ("row", "place")
ROW_ORDER = (2, 3, 0, 1)
PLACE_ORDER = (4, 3, 5, 2, 6, 1, 7, 0)
FAR_ORDER = (2, 0, 3, 1)
LATE = 2
HEAD_ORDER = (4, 5, 2, 3, 0, 1, 6, 7)
NEAR_ORDER = [r * OCT + p for r in ROW_ORDER for p in PLACE_ORDER]
RETURN_PLACES = (5, 4, 6, 3, 7, 2, 1, 0)
RETURN_ORDER = [r * OCT + p for r in ROW_ORDER for p in RETURN_PLACES]
SLICE_AT = [RETURN_ORDER.index(d) for d in NEAR_ORDER]
BF16, F32 = jnp.bfloat16, jnp.float32
VMEM = pl.BlockSpec(memory_space=pltpu.VMEM)
HBM = pl.BlockSpec(memory_space=pl.ANY)


def dot(a, b, left, right):
    return lax.dot_general(a, b, (((left,), (right,)), ((), ())), preferred_element_type=F32)


def local_terms(scale, q, k, v, g):
    shape = (q.shape[0], q.shape[0])
    seen = lax.broadcasted_iota(jnp.int32, shape, 0) >= lax.broadcasted_iota(jnp.int32, shape, 1)
    probs = jnp.where(seen, dot(q, k, 1, 1) * scale, 0.0).astype(BF16)
    dprobs = jnp.where(seen, dot(g, v, 1, 1) * scale, 0.0).astype(BF16)
    return dot(dprobs, k, 1, 0), dot(dprobs, q, 0, 0), dot(probs, g, 0, 0)


def block_kernel(scale, q_in, k_in, v_in, g_in, pieces_ref, *rest):
    grads, (q_ref, k_ref, v_ref, g_ref), sems = rest[:3], rest[3:7], rest[7]
    copies = [
        pltpu.make_async_copy(src, dst, sems.at[n])
        for n, (src, dst) in enumerate(((k_in, k_ref), (v_in, v_ref), (q_in, q_ref), (g_in, g_ref)))
    ]
    for copy in copies:
        copy.start()
    heads, parts = q_ref.shape[1] // DH, DH // 8
    for half, (a_ref, b_ref) in enumerate(((k_ref, v_ref), (q_ref, g_ref))):
        copies[2 * half].wait()
        copies[2 * half + 1].wait()
        for h in range(heads):
            cols = pl.ds(h * DH, DH)
            out = dot(a_ref[:, cols], b_ref[:, cols], 0, 0)
            pieces_ref[h * parts : (h + 1) * parts, half] = out.reshape(parts, 8, DH).astype(BF16)

    @pl.when(lax.axis_index("oct") < LATE)
    def _():
        for h in range(heads):
            cols = pl.ds(h * DH, DH)
            terms = local_terms(scale, q_ref[:, cols], k_ref[:, cols], v_ref[:, cols], g_ref[:, cols])
            for ref, term in zip(grads, terms):
                ref[:, cols] = term


def totals_kernel(pieces_ref, sends_ref):
    mine = lax.axis_index("oct")
    kv, qg = [None] * ROWS, [None] * ROWS
    for i, row in enumerate(ROW_ORDER):
        kv[row] = jnp.sum(pieces_ref[i * OCT : (i + 1) * OCT, 0].astype(F32), axis=0)
        qg[row] = jnp.sum(pieces_ref[i * OCT : (i + 1) * OCT, 1].astype(F32), axis=0)
    kv_up, qg_down = kv[:1], qg[-1:]
    for row in range(1, ROWS):
        kv_up.append(kv_up[-1] + kv[row])
        qg_down.insert(0, qg[ROWS - 1 - row] + qg_down[0])
    to_later = [a.astype(BF16) for a in kv_up + qg_down[1:]]
    to_earlier = [a.astype(BF16) for a in kv_up[:-1] + qg_down]
    for s, z in enumerate(FAR_ORDER):
        @pl.when(mine < z)
        def _():
            for n, a in enumerate(to_later):
                sends_ref[s, n] = a

        @pl.when(mine >= z)
        def _():
            for n, a in enumerate(to_earlier):
                sends_ref[s, n] = a


def prefix_kernel(scale, far_ref, pieces_ref, back_ref):
    mine = lax.axis_index("oct")
    kv_far, qg_far = [0.0] * ROWS, [0.0] * ROWS
    for s, z in enumerate(FAR_ORDER):
        slots = [far_ref[s, n].astype(F32) for n in range(2 * ROWS - 1)]
        earlier, later = z < mine, z > mine
        for row in range(ROWS):
            kv = jnp.where(earlier, slots[row], 0.0)
            qg = jnp.where(later, slots[ROWS - 1 + row], 0.0)
            if row > 0:
                kv = jnp.where(later, slots[row - 1], kv)
            if row < ROWS - 1:
                qg = jnp.where(earlier, slots[ROWS + row], qg)
            kv_far[row], qg_far[row] = kv_far[row] + kv, qg_far[row] + qg
    order = [ROW_ORDER.index(row) * OCT for row in range(ROWS)]
    own = 0.0
    for row in range(ROWS):
        for place in range(OCT):
            at = order[row] + PLACE_ORDER.index(place)
            back_ref[order[row] + RETURN_PLACES.index(place), 0] = ((kv_far[row] + own) * scale).astype(BF16)
            own = own + pieces_ref[at, 0].astype(F32)
    own = 0.0
    for row in reversed(range(ROWS)):
        for place in reversed(range(OCT)):
            at = order[row] + PLACE_ORDER.index(place)
            back_ref[order[row] + RETURN_PLACES.index(place), 1] = ((qg_far[row] + own) * scale).astype(BF16)
            own = own + pieces_ref[at, 1].astype(F32)


def combine_kernel(scale, back_ref, q_ref, k_ref, v_ref, g_ref, dq_ref, dk_ref, dv_ref, packed_ref):
    tokens, width = k_ref.shape
    parts = DH // 8
    groups, own = packed_ref.shape[0], packed_ref.shape[1] // 3

    def head(h, local):
        cols = pl.ds(h * DH, DH)
        k, v, g = k_ref[:, cols], v_ref[:, cols], g_ref[:, cols]
        state, later = (
            jnp.concatenate([back_ref[at, half].astype(F32) for at in SLICE_AT[h * parts : (h + 1) * parts]]).astype(BF16)
            for half in range(2)
        )
        far = dot(g, state, 1, 1), dot(v, later, 1, 1), dot(k, later, 1, 0)
        for n, (a, b) in enumerate(zip(local, far)):
            out = (a + b).reshape(groups, own, DH).astype(BF16)
            for i, j in enumerate(HEAD_ORDER):
                packed_ref[i, n * own : (n + 1) * own, cols] = out[j]

    late = lax.axis_index("oct") >= LATE

    @pl.when(late)
    def _():
        for h in range(width // DH):
            cols = pl.ds(h * DH, DH)
            head(h, local_terms(scale, q_ref[:, cols], k_ref[:, cols], v_ref[:, cols], g_ref[:, cols]))

    @pl.when(jnp.logical_not(late))
    def _():
        for h in range(width // DH):
            cols = pl.ds(h * DH, DH)
            head(h, (dq_ref[:, cols], dk_ref[:, cols], dv_ref[:, cols]))


def spread_kernel(packed_ref, oq_ref, ok_ref, ov_ref, buf, sems):
    groups, rows, width = packed_ref.shape
    own = rows // 3
    copies = []
    for n, out in enumerate((oq_ref, ok_ref, ov_ref)):
        for i, j in enumerate(HEAD_ORDER):
            buf[n, :, j * width : (j + 1) * width] = packed_ref[i, n * own : (n + 1) * own, :]
        copy = pltpu.make_async_copy(buf.at[n], out, sems.at[n])
        copy.start()
        copies.append(copy)
    for copy in copies:
        copy.wait()


def inv(x):
    return pltpu.with_memory_space_constraint(x, pltpu.VMEM)


def call(kernel, ins, outs, in_specs=None, out_specs=None, **kw):
    return pl.pallas_call(
        kernel,
        out_shape=outs,
        in_specs=in_specs or [VMEM] * len(ins),
        out_specs=out_specs or jax.tree.map(lambda _: VMEM, outs),
        **kw,
    )(*ins)


def on_device(q, k, v, g):
    tokens, width = q.shape
    heads = width // DH
    length = tokens * ROWS * OCTS * OCT
    scale = 1.0 / math.sqrt(DH * length)
    near = ROWS * OCT
    shape = lambda s, t: jax.ShapeDtypeStruct(s, t)
    vshape = lambda s, t: pltpu.VMEM(s, t)

    local, bf = vshape((tokens, width), F32), vshape((tokens, width), BF16)
    pieces, dq, dk, dv, q, k, v, g = call(
        functools.partial(block_kernel, scale),
        (q, k, v, g),
        (vshape((near, 2, 8, DH), BF16),) + (local,) * 3 + (bf,) * 4,
        in_specs=[HBM] * 4,
        scratch_shapes=[pltpu.SemaphoreType.DMA((4,))],
    )
    with jax.named_scope("near_exchange"):
        pieces = lax.all_to_all(pieces, NEAR, 0, 0, tiled=True, axis_index_groups=[NEAR_ORDER])
    sends = call(totals_kernel, (inv(pieces),), vshape((OCTS, 2 * ROWS - 1, 8, DH), BF16))
    with jax.named_scope("far_exchange"):
        far = lax.all_to_all(sends, "oct", 0, 0, tiled=True, axis_index_groups=[FAR_ORDER])
    back = call(
        functools.partial(prefix_kernel, scale),
        (inv(far), inv(pieces)),
        vshape((near, 2, 8, DH), BF16),
    )
    with jax.named_scope("near_return"):
        back = lax.all_to_all(back, NEAR, 0, 0, tiled=True, axis_index_groups=[RETURN_ORDER])
    groups = lax.axis_size(("x", "core"))
    own = tokens // groups
    packed = call(functools.partial(combine_kernel, scale), tuple(map(inv, (back, q, k, v, g, dq, dk, dv))), vshape((groups, 3 * own, width), BF16))
    with jax.named_scope("heads_to_tokens"):
        packed = lax.all_to_all(packed, ("x", "core"), 0, 0, tiled=True, axis_index_groups=[HEAD_ORDER])
    out = shape((own, groups * width), BF16)
    return call(
        spread_kernel,
        (inv(packed),),
        (out,) * 3,
        out_specs=(HBM,) * 3,
        scratch_shapes=[pltpu.VMEM((3, own, groups * width), BF16), pltpu.SemaphoreType.DMA((3,))],
    )


def solution(mesh):
    split = Mesh(
        np.asarray(mesh.devices).reshape(ROWS, OCTS, OCT, 4, 2),
        ("row", "oct", "place", "x", "core"),
    )
    seq, head = ("row", "oct", "place"), ("x", "core")
    return jax.shard_map(
        on_device,
        mesh=split,
        in_specs=(P(seq, head),) * 4,
        out_specs=(P(seq + head, None),) * 3,
        check_vma=False,
    )
```
